32 devices in a mesh: groups: 2 (over x), chan: 16 (over z, y, core).
Axes of the slice: x: 2, y: 2, z: 4, core: 2. Of those that a mesh axis runs over, the one named last changes fastest.
Arguments:
- spectra: bfloat16 [2, 8, 512, 512], P(None, 'groups', 'chan'), parts along dimension 1, may hold values from -6 to 6
- filter_bank: float32 [2, 8, 65], replicated, may hold values from -0.5 to 0.5
- band_index: int32 [512], replicated, may hold values from 0 to 7
- window_mask: int32 [8, 512], P('groups', 'chan'), parts along dimension 0, may hold values 0 or 1
- owner_order: int32 [8], P('groups'), parts along dimension 0, may hold values from 0 to 15, as said below
- source_offset: int32 [8, 32], P('groups'), parts along dimension 0, may hold values from 0 to 31, each once within a row
Outputs:
- cross: bfloat16 [2, 256, 512, 512], P(None, 'groups', 'chan'), parts along dimension 1
The draws below stay inside these ranges and needn't reach their ends.
There are 2 independent parts, one for each index of `groups`. The reference program is written for one: setup_inputs(seed, part) draws one part's arguments, and reference() takes and returns one part's arrays. A program takes and returns all parts, laid end to end along the dimension named above; an argument that names none is the same for every part. Nothing has to cross between parts.
Inputs may be any that keep to these rules, and one draw needn't show every extreme that they name: `owner_order`: 4 distinct device indices, below 16.
All inputs are finite; a program needn't handle non-finite values. No bound on the sum of `window_mask` on one device may be relied on, other than what follows from the above.
Results may differ from the reference program's by a relative error of at most 0.0057.
Values may be sent and summed in bfloat16 or wider, within the bound.
A program may use at most 192 MiB of HBM per device.

```python
import jax
import jax.numpy as jnp
from jax import lax

F = 512
CH_DEV = 32
WIN = 4
TAPS = 65
NBANK = 8
SMOOTH = 17
ROUNDS = 4
CHANNELS = 512
N_CHAN = 16


def draw_owner_order(key, part):
    devices = CHANNELS // CH_DEV
    first, second = jax.random.split(key)
    middle = 1 + jax.random.permutation(first, devices - 2)[:ROUNDS - 2]
    chosen = jnp.concatenate([jnp.array([0, devices - 1], jnp.int32), middle.astype(jnp.int32)])
    order = jax.random.permutation(second, ROUNDS)
    return chosen[order].astype(jnp.int32)


def plant(entries, key, least, largest):
    index_at = [jax.random.randint(jax.random.fold_in(key, axis), (), 0, length) for axis, length in enumerate(entries.shape)]
    longest = entries.shape.index(max(entries.shape))
    beside = index_at[:longest] + [(index_at[longest] + 1) % entries.shape[longest]] + index_at[longest + 1:]
    return entries.at[tuple(index_at)].set(least).at[tuple(beside)].set(largest)


def level_of(stream_key, dims, cuts, smallest, top_value):
    def one(dim, parts):
        steps = jax.random.uniform(jax.random.fold_in(jax.random.fold_in(stream_key, 6), dim), (parts,), jnp.float32, smallest / len(cuts), top_value / len(cuts))
        return jnp.repeat(jnp.exp(steps), dims[dim] // parts).reshape((-1,) + (1,) * (len(dims) - dim - 1))

    factor_of = one(*cuts[0])
    for cut in cuts[1:]:
        factor_of = factor_of * one(*cut)
    return factor_of


def gaussian(key, dims, deviation, limit, cuts=(), kind=jnp.bfloat16):
    entries = jax.random.normal(key, dims, jnp.float32) * deviation
    if len(cuts) > 0:
        entries = level_of(key, dims, cuts, -0.22, 0.18) * entries
    return jnp.clip(entries, min=-limit, max=limit).astype(kind)


def setup_inputs(seed: int = 0, part: int = 0) -> dict:
    key_of = jax.random.split(jax.random.key(seed), 7)
    part_splits = jax.random.split(jax.random.fold_in(key_of[6], part), 7)
    return {
        "spectra": gaussian(part_splits[0], (2, WIN, CHANNELS, F), 1.0, 6.0, ((2, 16),)),
        "filter_bank": gaussian(key_of[1], (2, NBANK, TAPS), (2 * TAPS) ** -0.5, 0.5, (), jnp.float32),
        "band_index": plant(jax.random.randint(key_of[2], (F,), 0, NBANK), jax.random.fold_in(key_of[2], 1), 0, NBANK - 1).astype(jnp.int32),
        "window_mask": plant((jax.random.randint(part_splits[3], (WIN, CHANNELS), 0, 8) < 7).astype(jnp.int32), jax.random.fold_in(part_splits[3], 1), 0, 1),
        "owner_order": draw_owner_order(jax.random.fold_in(jax.random.fold_in(key_of[6], part), 71), part),
        "source_offset": jax.vmap(lambda own: jax.random.permutation(own, CH_DEV))(jax.random.split(part_splits[5], ROUNDS)).reshape((ROUNDS, CH_DEV)).astype(jnp.int32),
    }


water_level = 0.05

def filter_taps(filter_bank, band_index):
    choose = (band_index[:, None] == jnp.arange(NBANK, dtype=jnp.int32)[None, :]).astype(jnp.float32)
    return jnp.einsum('fb,pbk->pkf', choose, filter_bank, precision=lax.Precision.HIGHEST)

def velocity_whiten(padded, taps, window_mask):
    count = padded.shape[2] - (TAPS - 1)
    real_sum = jnp.zeros((padded.shape[1], count, padded.shape[3]), jnp.float32)
    imag_sum = jnp.zeros((padded.shape[1], count, padded.shape[3]), jnp.float32)
    for tap_pos in range(TAPS):
        real_in = padded[0, :, tap_pos:tap_pos + count]
        imag_in = padded[1, :, tap_pos:tap_pos + count]
        real_sum = real_sum + taps[0, tap_pos] * real_in - taps[1, tap_pos] * imag_in
        imag_sum = imag_sum + taps[0, tap_pos] * imag_in + taps[1, tap_pos] * real_in
    power = real_sum * real_sum + imag_sum * imag_sum
    reach = SMOOTH // 2
    padded_power = jnp.pad(power, ((0, 0), (0, 0), (reach, reach)))
    smooth = jnp.zeros_like(power)
    for shift_pos in range(SMOOTH):
        smooth = smooth + padded_power[:, :, shift_pos:shift_pos + power.shape[2]]
    smooth = smooth / SMOOTH
    scale = lax.rsqrt(smooth + water_level) * window_mask.astype(jnp.float32)[:, :, None]
    return jnp.stack([real_sum * scale, imag_sum * scale]).astype(jnp.bfloat16)

def cross_block(source, whitened):
    src_real = source[0].astype(jnp.float32)
    src_imag = source[1].astype(jnp.float32)
    loc_real = whitened[0].astype(jnp.float32)
    loc_imag = whitened[1].astype(jnp.float32)
    real_out = jnp.einsum('wsf,wcf->scf', src_real, loc_real) + jnp.einsum('wsf,wcf->scf', src_imag, loc_imag)
    imag_out = jnp.einsum('wsf,wcf->scf', src_real, loc_imag) - jnp.einsum('wsf,wcf->scf', src_imag, loc_real)
    return (jnp.stack([real_out, imag_out]) / WIN).astype(jnp.bfloat16)

def reference(spectra, filter_bank, band_index, window_mask, owner_order, source_offset):
    half_width = TAPS // 2
    taps = filter_taps(filter_bank, band_index)
    padded = jnp.pad(spectra.astype(jnp.float32), ((0, 0), (0, 0), (half_width, half_width), (0, 0)))
    whitened = velocity_whiten(padded, taps, window_mask)
    channel_index = (owner_order[:, None] * CH_DEV + source_offset).reshape(-1).astype(jnp.int32)
    picked = whitened[:, :, channel_index, :]
    picked = picked.reshape(2, WIN, ROUNDS, CH_DEV, F).transpose(2, 0, 1, 3, 4)
    blocks = lax.map(lambda source: cross_block(source, whitened), picked)
    return blocks.transpose(1, 0, 2, 3, 4).reshape(2, ROUNDS * CH_DEV, CH_DEV * N_CHAN, F)
```

```python
import functools

import jax
import jax.numpy as jnp
from jax import lax
from jax.experimental import pallas as pl
from jax.experimental.pallas import tpu as pltpu
from jax.sharding import PartitionSpec as P

SMOOTH = 17
water_level = 0.05
bf16 = jnp.bfloat16
f32 = jnp.float32
LANES = 128


def split(x):
    hi = x.astype(bf16)
    return hi, (x - hi.astype(f32)).astype(bf16)


def build_toeplitz(bank_ref, toep):
    _, nbank, ntap = bank_ref.shape
    chans = toep.shape[1] // (2 * nbank)
    for b in range(nbank):
        parts = []
        for p in range(2):
            row = jnp.concatenate(
                [bank_ref[p, b : b + 1, :], jnp.zeros((1, LANES - ntap), f32)], axis=1
            )
            full = jnp.broadcast_to(row, (chans, LANES))
            parts.append(split(pltpu.roll(full, 0, 1, stride=1, stride_axis=0)))
        at = b * 2 * chans
        for part in range(2):
            real, imag = parts[0][part], parts[1][part]
            toep[part, at : at + chans, :LANES] = real
            toep[part, at : at + chans, LANES:] = -imag
            toep[part, at + chans : at + 2 * chans, :LANES] = imag
            toep[part, at + chans : at + 2 * chans, LANES:] = real


def build_window(band):
    bins = band.shape[0]
    rows = lax.broadcasted_iota(jnp.int32, (bins, bins), 0)
    cols = lax.broadcasted_iota(jnp.int32, (bins, bins), 1)
    band[...] = (jnp.abs(rows - cols) <= SMOOTH // 2).astype(f32).astype(bf16)


def filter_whiten(nbank, xs, toep, band, index_ref, mask_ref, filt, power, out_ref):
    wins, chans = mask_ref.shape
    bins = band.shape[0]
    tile = 256
    for w in range(wins):
        for n in range(bins // tile):
            cut = slice(n * tile, (n + 1) * tile)
            x = xs[w, :, cut]
            res = jnp.dot(toep[0], x, preferred_element_type=f32)
            res += jnp.dot(toep[1], x, preferred_element_type=f32)
            index = index_ref[:, cut]
            acc = res[: 2 * chans]
            for b in range(1, nbank):
                acc = jnp.where(index == b, res[2 * chans * b : 2 * chans * (b + 1)], acc)
            real, imag = acc[:chans], acc[chans:]
            rows = slice(w * chans, (w + 1) * chans)
            filt[0, rows, cut] = real
            filt[1, rows, cut] = imag
            hi, lo = split(real * real + imag * imag)
            power[0, rows, cut] = hi
            power[1, rows, cut] = lo
    smooth = jnp.dot(power[0], band[...], preferred_element_type=f32)
    smooth += jnp.dot(power[1], band[...], preferred_element_type=f32)
    scale = lax.rsqrt(smooth * (1.0 / SMOOTH) + water_level)
    eye = lax.broadcasted_iota(jnp.int32, (chans, chans), 0) == lax.broadcasted_iota(
        jnp.int32, (chans, chans), 1
    )
    for w in range(wins):
        row = jnp.broadcast_to(mask_ref[w : w + 1, :].astype(f32), (chans, chans))
        valid = jnp.sum(jnp.where(eye, row, 0.0), axis=1, keepdims=True)
        rows = slice(w * chans, (w + 1) * chans)
        here = scale[rows] * valid
        for p in range(2):
            out_ref[p, w] = (filt[p, rows] * here).astype(bf16)


def whiten_kernel(
    left_ref, own_ref, right_ref, bank_ref, index_ref, mask_ref, out_ref, xs, toep, band, filt, power
):
    wins, chans = mask_ref.shape
    build_toeplitz(bank_ref, toep)
    build_window(band)
    for p in range(2):
        for w in range(wins):
            at = p * LANES
            xs[w, at : at + chans] = left_ref[p, w]
            xs[w, at + chans : at + 2 * chans] = own_ref[p, w]
            xs[w, at + 2 * chans : at + 3 * chans] = right_ref[p, w]
            xs[w, at + 3 * chans : at + LANES] = jnp.zeros((LANES - 3 * chans, xs.shape[2]), bf16)
    filter_whiten(bank_ref.shape[1], xs, toep, band, index_ref, mask_ref, filt, power, out_ref)


def whiten(left, own, right, bank, index, mask):
    _, wins, chans, bins = own.shape
    nbank = bank.shape[1]
    return pl.pallas_call(
        whiten_kernel,
        out_shape=jax.ShapeDtypeStruct(own.shape, bf16),
        in_specs=[pl.BlockSpec(memory_space=pltpu.VMEM)] * 6,
        out_specs=pl.BlockSpec(memory_space=pltpu.VMEM),
        scratch_shapes=[
            pltpu.VMEM((wins, 2 * LANES, bins), bf16),
            pltpu.VMEM((2, nbank * 2 * chans, 2 * LANES), bf16),
            pltpu.VMEM((bins, bins), bf16),
            pltpu.VMEM((2, wins * chans, bins), f32),
            pltpu.VMEM((2, wins * chans, bins), bf16),
        ],
        name="whiten",
    )(left, own, right, bank, index, mask)


def tree_sum(terms):
    while len(terms) > 1:
        terms = [a + b for a, b in zip(terms[::2], terms[1::2])]
    return terms[0]


def cross_kernel(offset_ref, src_ref, loc_ref, out_ref, wide):
    _, wins, chans, bins = loc_ref.shape
    count = out_ref.shape[1]
    r, h = pl.program_id(0), pl.program_id(1)

    @pl.when(h == 0)
    def _():
        for p in range(2):
            for w in range(wins):
                wide[:, p * wins + w, :] = src_ref[0, p, w].astype(f32) * (1.0 / wins)

    for n in range(bins // LANES):
        cut = slice(n * LANES, (n + 1) * LANES)
        loc = [[loc_ref[p, w, :, cut] for w in range(wins)] for p in range(2)]

        def one(j, carry, cut=cut, loc=loc):
            at = offset_ref[r, h * count + j]
            src = [
                [
                    jnp.broadcast_to(
                        wide[at, p * wins + w : p * wins + w + 1, cut], (chans, LANES)
                    ).astype(bf16)
                    for w in range(wins)
                ]
                for p in range(2)
            ]
            real = tree_sum(
                [src[p][w] * loc[p][w] for w in range(wins) for p in range(2)]
            )
            plus = tree_sum([src[0][w] * loc[1][w] for w in range(wins)])
            minus = tree_sum([src[1][w] * loc[0][w] for w in range(wins)])
            out_ref[0, j, :, cut] = real
            out_ref[1, j, :, cut] = plus - minus
            return carry

        lax.fori_loop(0, count, one, 0, unroll=4)


def cross(offset, src, loc, blocks=2):
    rounds, _, wins, chans, bins = src.shape
    per = chans // blocks
    return pl.pallas_call(
        cross_kernel,
        out_shape=jax.ShapeDtypeStruct((2, rounds * chans, chans, bins), bf16),
        grid=(rounds, blocks),
        in_specs=[
            pl.BlockSpec(memory_space=pltpu.SMEM),
            pl.BlockSpec((1, 2, wins, chans, bins), lambda r, h: (r, 0, 0, 0, 0)),
            pl.BlockSpec((2, wins, chans, bins), lambda r, h: (0, 0, 0, 0)),
        ],
        out_specs=pl.BlockSpec((2, per, chans, bins), lambda r, h: (0, r * blocks + h, 0, 0)),
        scratch_shapes=[pltpu.VMEM((chans, 2 * wins, bins), f32)],
        name="cross",
    )(offset, src, loc)


def body(spectra, filter_bank, band_index, window_mask, owner_order, source_offset):
    count = lax.axis_size("chan")
    ends = count - 1
    left = lax.ppermute(spectra, "chan", [(i, i + 1) for i in range(ends)])
    right = lax.ppermute(spectra, "chan", [(i + 1, i) for i in range(ends)])
    whitened = whiten(left, spectra, right, filter_bank, band_index[None, :], window_mask)
    here = (lax.axis_index("chan") == owner_order)[:, None, None, None, None]
    stacked = jnp.where(here, whitened[None], jnp.zeros((), bf16))
    summed = lax.psum(stacked, "chan")
    return cross(source_offset, summed, whitened)


def solution(mesh):
    in_specs = (
        P(None, "groups", "chan", None),
        P(),
        P(),
        P("groups", "chan"),
        P("groups"),
        P("groups", None),
    )
    out_specs = P(None, "groups", "chan", None)
    return jax.shard_map(body, mesh=mesh, in_specs=in_specs, out_specs=out_specs, check_vma=False)
```

```python
import functools

import jax
import jax.numpy as jnp
from jax import lax
from jax.experimental import pallas as pl
from jax.experimental.pallas import tpu as pltpu
from jax.sharding import PartitionSpec as P

SMOOTH = 17
water_level = 0.05
bf16 = jnp.bfloat16
f32 = jnp.float32
LANES = 128


def split(x):
    hi = x.astype(bf16)
    return hi, (x - hi.astype(f32)).astype(bf16)


def build_toeplitz(bank_ref, toep):
    _, nbank, ntap = bank_ref.shape
    chans = toep.shape[1] // (2 * nbank)
    for b in range(nbank):
        parts = []
        for p in range(2):
            row = jnp.concatenate(
                [bank_ref[p, b : b + 1, :], jnp.zeros((1, LANES - ntap), f32)], axis=1
            )
            full = jnp.broadcast_to(row, (chans, LANES))
            parts.append(split(pltpu.roll(full, 0, 1, stride=1, stride_axis=0)))
        at = b * 2 * chans
        for part in range(2):
            real, imag = parts[0][part], parts[1][part]
            toep[part, at : at + chans, :LANES] = real
            toep[part, at : at + chans, LANES:] = -imag
            toep[part, at + chans : at + 2 * chans, :LANES] = imag
            toep[part, at + chans : at + 2 * chans, LANES:] = real


def build_window(band):
    bins = band.shape[0]
    rows = lax.broadcasted_iota(jnp.int32, (bins, bins), 0)
    cols = lax.broadcasted_iota(jnp.int32, (bins, bins), 1)
    band[...] = (jnp.abs(rows - cols) <= SMOOTH // 2).astype(f32).astype(bf16)


def filter_window(nbank, w, x, toep, index_ref, filt, power):
    bins = filt.shape[2]
    chans = toep.shape[1] // (2 * nbank)
    tile = 256
    rows = slice(w * chans, (w + 1) * chans)
    for n in range(bins // tile):
        cut = slice(n * tile, (n + 1) * tile)
        here = x(cut)
        res = jnp.dot(toep[0], here, preferred_element_type=f32)
        res += jnp.dot(toep[1], here, preferred_element_type=f32)
        index = index_ref[:, cut]
        acc = res[: 2 * chans]
        for b in range(1, nbank):
            acc = jnp.where(index == b, res[2 * chans * b : 2 * chans * (b + 1)], acc)
        real, imag = acc[:chans], acc[chans:]
        filt[0, rows, cut] = real
        filt[1, rows, cut] = imag
        hi, lo = split(real * real + imag * imag)
        power[0, rows, cut] = hi
        power[1, rows, cut] = lo


def whiten_window(w, band, mask_ref, filt, power):
    chans = mask_ref.shape[1]
    rows = slice(w * chans, (w + 1) * chans)
    smooth = jnp.dot(power[0, rows], band[...], preferred_element_type=f32)
    smooth += jnp.dot(power[1, rows], band[...], preferred_element_type=f32)
    scale = lax.rsqrt(smooth * (1.0 / SMOOTH) + water_level)
    eye = lax.broadcasted_iota(jnp.int32, (chans, chans), 0) == lax.broadcasted_iota(
        jnp.int32, (chans, chans), 1
    )
    row = jnp.broadcast_to(mask_ref[w : w + 1, :].astype(f32), (chans, chans))
    valid = jnp.sum(jnp.where(eye, row, 0.0), axis=1, keepdims=True)
    scale = scale * valid
    return [(filt[p, rows] * scale).astype(bf16) for p in range(2)]


class Line:
    def __init__(self, pos, length, device_of, lead, refs):
        self.pos, self.length, self.device_of, self.lead = pos, length, device_of, lead
        self.own, self.out_r, self.out_l, self.in_r, self.in_l, self.sems = refs
        self.count = self.own.shape[0]

    def clear(self):
        @pl.when(self.pos == 0)
        def _():
            self.in_r[...] = jnp.zeros_like(self.in_r)

        @pl.when(self.pos == self.length - 1)
        def _():
            self.in_l[...] = jnp.zeros_like(self.in_l)

    def copy(self, way, k):
        out, into = (self.out_r, self.in_r) if way == 0 else (self.out_l, self.in_l)
        other = self.pos + 1 if way == 0 else self.pos - 1
        return pltpu.make_async_remote_copy(
            src_ref=out.at[k],
            dst_ref=into.at[k],
            send_sem=self.sems.at[way, 0, k],
            recv_sem=self.sems.at[way, 1, k],
            device_id={"chan": self.device_of(other)},
            device_id_type=pl.DeviceIdType.MESH,
        )

    def tick(self, t):
        for way in range(2):
            behind = self.pos if way == 0 else self.length - 1 - self.pos
            out, into = (self.out_r, self.in_r) if way == 0 else (self.out_l, self.in_l)
            k = t - self.lead - behind
            inside = jnp.logical_and(k >= 0, k < self.count)

            @pl.when(jnp.logical_and(inside, behind > 0))
            def _(way=way, k=k):
                self.copy(way, k).wait_recv()

            @pl.when(jnp.logical_and(inside, behind < self.length - 1))
            def _(way=way, k=k, out=out, into=into):
                out[k] = self.own[k] + into[k]
                self.copy(way, k).start()

    def result(self, k):
        return self.own[k] + self.in_r[k] + self.in_l[k]

    def drain(self):
        for way in range(2):
            behind = self.pos if way == 0 else self.length - 1 - self.pos

            @pl.when(behind < self.length - 1)
            def _(way=way):
                @pl.loop(0, self.count)
                def _(k):
                    self.copy(way, k).wait_send()


def front_kernel(
    rows,
    cols,
    owner_ref,
    own_ref,
    bank_ref,
    index_ref,
    mask_ref,
    out_ref,
    src_ref,
    halo,
    toep,
    band,
    filt,
    power,
    mine,
    paired,
    col_buf,
    row_buf,
    done,
    other,
    halo_sems,
    pair_sems,
    col_sems,
    row_sems,
    done_sems,
):
    wins, chans = mask_ref.shape
    bins = own_ref.shape[3]
    half = wins // 2
    me = lax.axis_index("chan")
    size = rows * cols * 2
    core = me % 2
    col = (me // 2) % cols
    row = me // (2 * cols)
    partner = me + 1 - 2 * core
    mesh_id = pl.DeviceIdType.MESH

    barrier = pltpu.get_barrier_semaphore()
    partners = [
        (me > 0, me - 1),
        (me < size - 1, me + 1),
        (me >= 0, partner),
        (col > 0, me - 2),
        (col < cols - 1, me + 2),
        (row > 0, me - 2 * cols),
        (row < rows - 1, me + 2 * cols),
    ]
    expected = jnp.int32(0)
    for there, who in partners:
        expected += there.astype(jnp.int32)

        @pl.when(there)
        def _(who=who):
            pl.semaphore_signal(barrier, inc=1, device_id={"chan": who}, device_id_type=mesh_id)

    pl.semaphore_wait(barrier, expected)

    def halo_copy(way, w):
        return pltpu.make_async_remote_copy(
            src_ref=own_ref.at[:, w],
            dst_ref=halo.at[way, :, w],
            send_sem=halo_sems.at[way, 0, w],
            recv_sem=halo_sems.at[way, 1, w],
            device_id={"chan": me + 1 - 2 * way},
            device_id_type=mesh_id,
        )

    sends = (me < size - 1, me > 0)
    for w in range(wins):
        for way in range(2):

            @pl.when(sends[way])
            def _(way=way, w=w):
                halo_copy(way, w).start()

    for way in range(2):

        @pl.when(jnp.logical_not(sends[1 - way]))
        def _(way=way):
            halo[way] = jnp.zeros_like(halo[way])

    line_col = Line(col, cols, lambda i: (row * cols + i) * 2 + core, 0, (*col_buf, col_sems))
    line_row = Line(row, rows, lambda i: (i * cols + col) * 2 + core, cols - 1, (*row_buf, row_sems))
    line_col.clear()
    line_row.clear()
    build_toeplitz(bank_ref, toep)
    build_window(band)

    blank = jnp.zeros((LANES - 3 * chans, bins), bf16)
    for w in range(wins):
        for way in range(2):

            @pl.when(sends[1 - way])
            def _(way=way, w=w):
                halo_copy(way, w).wait_recv()

        def x(cut, w=w):
            parts = []
            for p in range(2):
                parts += [halo[0, p, w, :, cut], own_ref[p, w, :, cut], halo[1, p, w, :, cut]]
                parts += [blank[:, cut]]
            return jnp.concatenate(parts, axis=0)

        filter_window(bank_ref.shape[1], w, x, toep, index_ref, filt, power)
    for w in range(wins):
        white = whiten_window(w, band, mask_ref, filt, power)
        for p in range(2):
            out_ref[p, w] = white[p]
            mine[w, p] = white[p]

    pair = pltpu.make_async_remote_copy(
        src_ref=mine.at[pl.ds((1 - core) * half, half)],
        dst_ref=paired,
        send_sem=pair_sems.at[0],
        recv_sem=pair_sems.at[1],
        device_id={"chan": partner},
        device_id_type=mesh_id,
    )
    pair.start()
    pair.wait_recv()

    count = line_col.count
    own = col_buf[0]

    @pl.loop(0, count)
    def _(k):
        r, w = k // half, k % half
        first = (owner_ref[r] == me).astype(f32).astype(bf16)
        second = (owner_ref[r] == partner).astype(f32).astype(bf16)
        own[k] = mine[core * half + w] * first + paired[w] * second

    def done_copy(k):
        return pltpu.make_async_remote_copy(
            src_ref=done.at[k],
            dst_ref=other.at[k],
            send_sem=done_sems.at[0, k],
            recv_sem=done_sems.at[1, k],
            device_id={"chan": partner},
            device_id_type=mesh_id,
        )

    @pl.loop(0, count + cols + rows - 2)
    def _(t):
        k = t - (cols - 1)
        line_col.tick(t)

        @pl.when(jnp.logical_and(k >= 0, k < count))
        def _():
            line_row.own[k] = line_col.result(k)

        line_row.tick(t)
        last = t - (cols - 1) - (rows - 1)

        @pl.when(jnp.logical_and(last >= 0, last < count))
        def _():
            total = line_row.result(last)
            done[last] = total
            done_copy(last).start()
            for p in range(2):
                src_ref[last // half, p, core * half + last % half] = total[p]

    @pl.loop(0, count)
    def _(k):
        done_copy(k).wait_recv()
        for p in range(2):
            src_ref[k // half, p, (1 - core) * half + k % half] = other[k, p]

    for way in range(2):
        for w in range(wins):

            @pl.when(sends[way])
            def _(way=way, w=w):
                halo_copy(way, w).wait_send()

    pair.wait_send()
    line_col.drain()
    line_row.drain()

    @pl.loop(0, count)
    def _(k):
        done_copy(k).wait_send()


def front(grid, owner, own, bank, index, mask):
    _, wins, chans, bins = own.shape
    nbank = bank.shape[1]
    rounds = owner.shape[0]
    rows, cols = grid
    half = wins // 2
    count = rounds * half
    vmem = pl.BlockSpec(memory_space=pltpu.VMEM)
    chunk = (2, chans, bins)
    chunks = pltpu.VMEM((count, *chunk), bf16)
    return pl.pallas_call(
        functools.partial(front_kernel, rows, cols),
        out_shape=[
            jax.ShapeDtypeStruct(own.shape, bf16),
            jax.ShapeDtypeStruct((rounds, *own.shape), bf16),
        ],
        in_specs=[pl.BlockSpec(memory_space=pltpu.SMEM)] + [vmem] * 4,
        out_specs=[vmem] * 2,
        scratch_shapes=[
            pltpu.VMEM((2, *own.shape), bf16),
            pltpu.VMEM((2, nbank * 2 * chans, 2 * LANES), bf16),
            pltpu.VMEM((bins, bins), bf16),
            pltpu.VMEM((2, wins * chans, bins), f32),
            pltpu.VMEM((2, wins * chans, bins), bf16),
            pltpu.VMEM((wins, *chunk), bf16),
            pltpu.VMEM((half, *chunk), bf16),
            [chunks] * 5,
            [chunks] * 5,
            chunks,
            chunks,
            pltpu.SemaphoreType.DMA((2, 2, wins)),
            pltpu.SemaphoreType.DMA((2,)),
            pltpu.SemaphoreType.DMA((2, 2, count)),
            pltpu.SemaphoreType.DMA((2, 2, count)),
            pltpu.SemaphoreType.DMA((2, count)),
        ],
        compiler_params=pltpu.CompilerParams(collective_id=0, has_side_effects=True),
        name="front",
    )(owner, own, bank, index, mask)


def tree_sum(terms):
    while len(terms) > 1:
        terms = [a + b for a, b in zip(terms[::2], terms[1::2])]
    return terms[0]


def cross_kernel(offset_ref, src_ref, loc_ref, out_ref, wide):
    _, wins, chans, bins = loc_ref.shape
    count = out_ref.shape[1]
    r, h = pl.program_id(0), pl.program_id(1)

    @pl.when(h == 0)
    def _():
        for p in range(2):
            for w in range(wins):
                wide[:, p * wins + w, :] = src_ref[0, p, w].astype(f32) * (1.0 / wins)

    for n in range(bins // LANES):
        cut = slice(n * LANES, (n + 1) * LANES)
        loc = [[loc_ref[p, w, :, cut] for w in range(wins)] for p in range(2)]

        def one(j, carry, cut=cut, loc=loc):
            at = offset_ref[r, h * count + j]
            src = [
                [
                    jnp.broadcast_to(
                        wide[at, p * wins + w : p * wins + w + 1, cut], (chans, LANES)
                    ).astype(bf16)
                    for w in range(wins)
                ]
                for p in range(2)
            ]
            real = tree_sum(
                [src[p][w] * loc[p][w] for w in range(wins) for p in range(2)]
            )
            plus = tree_sum([src[0][w] * loc[1][w] for w in range(wins)])
            minus = tree_sum([src[1][w] * loc[0][w] for w in range(wins)])
            out_ref[0, j, :, cut] = real
            out_ref[1, j, :, cut] = plus - minus
            return carry

        lax.fori_loop(0, count, one, 0, unroll=4)


def cross(offset, src, loc, blocks=2):
    rounds, _, wins, chans, bins = src.shape
    per = chans // blocks
    return pl.pallas_call(
        cross_kernel,
        out_shape=jax.ShapeDtypeStruct((2, rounds * chans, chans, bins), bf16),
        grid=(rounds, blocks),
        in_specs=[
            pl.BlockSpec(memory_space=pltpu.SMEM),
            pl.BlockSpec((1, 2, wins, chans, bins), lambda r, h: (r, 0, 0, 0, 0)),
            pl.BlockSpec((2, wins, chans, bins), lambda r, h: (0, 0, 0, 0)),
        ],
        out_specs=pl.BlockSpec((2, per, chans, bins), lambda r, h: (0, r * blocks + h, 0, 0)),
        scratch_shapes=[pltpu.VMEM((chans, 2 * wins, bins), f32)],
        name="cross",
    )(offset, src, loc)


def chip_grid(size):
    chips = size // 2
    cols = 1
    while cols * cols * 4 <= chips:
        cols *= 2
    return chips // cols, cols


def body(spectra, filter_bank, band_index, window_mask, owner_order, source_offset):
    grid = chip_grid(lax.axis_size("chan"))
    whitened, sources = front(
        grid, owner_order, spectra, filter_bank, band_index[None, :], window_mask
    )
    return cross(source_offset, sources, whitened)


def solution(mesh):
    in_specs = (
        P(None, "groups", "chan", None),
        P(),
        P(),
        P("groups", "chan"),
        P("groups"),
        P("groups", None),
    )
    out_specs = P(None, "groups", "chan", None)
    return jax.shard_map(body, mesh=mesh, in_specs=in_specs, out_specs=out_specs, check_vma=False)
```

```python
import functools

import jax
import jax.numpy as jnp
from jax import lax
from jax.experimental import pallas as pl
from jax.experimental.pallas import tpu as pltpu
from jax.sharding import PartitionSpec as P

SMOOTH = 17
water_level = 0.05
bf16 = jnp.bfloat16
f32 = jnp.float32
LANES = 128
LAG = 4


def split(x):
    hi = x.astype(bf16)
    return hi, (x - hi.astype(f32)).astype(bf16)


def build_toeplitz(bank_ref, toep):
    _, nbank, ntap = bank_ref.shape
    chans = toep.shape[1] // (2 * nbank)
    for b in range(nbank):
        parts = []
        for p in range(2):
            row = jnp.concatenate(
                [bank_ref[p, b : b + 1, :], jnp.zeros((1, LANES - ntap), f32)], axis=1
            )
            full = jnp.broadcast_to(row, (chans, LANES))
            parts.append(split(pltpu.roll(full, 0, 1, stride=1, stride_axis=0)))
        at = b * 2 * chans
        for part in range(2):
            real, imag = parts[0][part], parts[1][part]
            toep[part, at : at + chans, :LANES] = real
            toep[part, at : at + chans, LANES:] = -imag
            toep[part, at + chans : at + 2 * chans, :LANES] = imag
            toep[part, at + chans : at + 2 * chans, LANES:] = real


def build_window(band):
    bins = band.shape[0]
    rows = lax.broadcasted_iota(jnp.int32, (bins, bins), 0)
    cols = lax.broadcasted_iota(jnp.int32, (bins, bins), 1)
    band[...] = (jnp.abs(rows - cols) <= SMOOTH // 2).astype(f32).astype(bf16)


def filter_window(nbank, w, x, toep, index_ref, filt, power):
    bins = filt.shape[2]
    chans = toep.shape[1] // (2 * nbank)
    tile = 256
    rows = slice(w * chans, (w + 1) * chans)
    for n in range(bins // tile):
        cut = slice(n * tile, (n + 1) * tile)
        here = x(cut)
        res = jnp.dot(toep[0], here, preferred_element_type=f32)
        res += jnp.dot(toep[1], here, preferred_element_type=f32)
        index = index_ref[:, cut]
        acc = res[: 2 * chans]
        for b in range(1, nbank):
            acc = jnp.where(index == b, res[2 * chans * b : 2 * chans * (b + 1)], acc)
        real, imag = acc[:chans], acc[chans:]
        filt[0, rows, cut] = real
        filt[1, rows, cut] = imag
        hi, lo = split(real * real + imag * imag)
        power[0, rows, cut] = hi
        power[1, rows, cut] = lo


def whiten_window(w, band, mask_ref, filt, power):
    chans = mask_ref.shape[1]
    rows = slice(w * chans, (w + 1) * chans)
    smooth = jnp.dot(power[0, rows], band[...], preferred_element_type=f32)
    smooth += jnp.dot(power[1, rows], band[...], preferred_element_type=f32)
    scale = lax.rsqrt(smooth * (1.0 / SMOOTH) + water_level)
    eye = lax.broadcasted_iota(jnp.int32, (chans, chans), 0) == lax.broadcasted_iota(
        jnp.int32, (chans, chans), 1
    )
    row = jnp.broadcast_to(mask_ref[w : w + 1, :].astype(f32), (chans, chans))
    valid = jnp.sum(jnp.where(eye, row, 0.0), axis=1, keepdims=True)
    scale = scale * valid
    return [(filt[p, rows] * scale).astype(bf16) for p in range(2)]


class Line:
    def __init__(self, pos, length, device_of, lag, refs):
        self.pos, self.length, self.device_of, self.lag = pos, length, device_of, lag
        self.own, self.out_r, self.out_l, self.in_r, self.in_l, self.sems = refs
        self.count = self.own.shape[0]

    def clear(self):
        @pl.when(self.pos == 0)
        def _():
            self.in_r[...] = jnp.zeros_like(self.in_r)

        @pl.when(self.pos == self.length - 1)
        def _():
            self.in_l[...] = jnp.zeros_like(self.in_l)

    def copy(self, way, k):
        out, into = (self.out_r, self.in_r) if way == 0 else (self.out_l, self.in_l)
        other = self.pos + 1 if way == 0 else self.pos - 1
        return pltpu.make_async_remote_copy(
            src_ref=out.at[k],
            dst_ref=into.at[k],
            send_sem=self.sems.at[way, 0, k],
            recv_sem=self.sems.at[way, 1, k],
            device_id={"chan": self.device_of(other)},
            device_id_type=pl.DeviceIdType.MESH,
        )

    def tick(self, t):
        for way in range(2):
            behind = self.pos if way == 0 else self.length - 1 - self.pos
            out, into = (self.out_r, self.in_r) if way == 0 else (self.out_l, self.in_l)
            k = t - self.lag * behind
            inside = jnp.logical_and(k >= 0, k < self.count)

            @pl.when(jnp.logical_and(inside, behind > 0))
            def _(way=way, k=k):
                self.copy(way, k).wait_recv()

            @pl.when(jnp.logical_and(inside, behind < self.length - 1))
            def _(way=way, k=k, out=out, into=into):
                out[k] = self.own[k] + into[k]
                self.copy(way, k).start()

    def result(self, k):
        return self.own[k] + self.in_r[k] + self.in_l[k]

    def drain(self):
        for way in range(2):
            behind = self.pos if way == 0 else self.length - 1 - self.pos

            @pl.when(behind < self.length - 1)
            def _(way=way):
                @pl.loop(0, self.count)
                def _(k):
                    self.copy(way, k).wait_send()


def front_kernel(
    rows,
    cols,
    owner_ref,
    own_ref,
    bank_ref,
    index_ref,
    mask_ref,
    out_ref,
    src_ref,
    halo,
    toep,
    band,
    filt,
    power,
    mine,
    beside,
    row_buf,
    done,
    other,
    halo_sems,
    beside_sems,
    row_sems,
    done_sems,
):
    wins, chans = mask_ref.shape
    bins = own_ref.shape[3]
    half = wins // 2
    rounds = src_ref.shape[0]
    me = lax.axis_index("chan")
    size = rows * cols * 2
    core = me % 2
    place = me % (2 * cols)
    base = me - place
    row = me // (2 * cols)
    partner = me + 1 - 2 * core
    mesh_id = pl.DeviceIdType.MESH

    barrier = pltpu.get_barrier_semaphore()
    partners = [
        (me > 0, me - 1),
        (me < size - 1, me + 1),
        (row > 0, me - 2 * cols),
        (row < rows - 1, me + 2 * cols),
    ] + [(place != j, base + j) for j in range(2 * cols)]
    expected = jnp.int32(0)
    for there, who in partners:
        expected += there.astype(jnp.int32)

        @pl.when(there)
        def _(who=who):
            pl.semaphore_signal(barrier, inc=1, device_id={"chan": who}, device_id_type=mesh_id)

    pl.semaphore_wait(barrier, expected)

    def halo_copy(way, w):
        return pltpu.make_async_remote_copy(
            src_ref=own_ref.at[:, w],
            dst_ref=halo.at[way, :, w],
            send_sem=halo_sems.at[way, 0, w],
            recv_sem=halo_sems.at[way, 1, w],
            device_id={"chan": me + 1 - 2 * way},
            device_id_type=mesh_id,
        )

    order = [c * half + w for w in range(half) for c in range(2)]
    sends = (me < size - 1, me > 0)
    for w in order:
        for way in range(2):

            @pl.when(sends[way])
            def _(way=way, w=w):
                halo_copy(way, w).start()

    for way in range(2):

        @pl.when(jnp.logical_not(sends[1 - way]))
        def _(way=way):
            halo[way] = jnp.zeros_like(halo[way])

    line = Line(row, rows, lambda i: i * 2 * cols + place, LAG, (*row_buf, row_sems))
    line.clear()
    build_toeplitz(bank_ref, toep)
    build_window(band)

    def beside_copy(sender, j, w):
        return pltpu.make_async_remote_copy(
            src_ref=mine.at[w],
            dst_ref=beside.at[sender, w % half],
            send_sem=beside_sems.at[0, j, w % half],
            recv_sem=beside_sems.at[1, sender, w % half],
            device_id={"chan": base + j},
            device_id_type=mesh_id,
        )

    blank = jnp.zeros((LANES - 3 * chans, bins), bf16)
    for w in order:
        for way in range(2):

            @pl.when(sends[1 - way])
            def _(way=way, w=w):
                halo_copy(way, w).wait_recv()

        def x(cut, w=w):
            parts = []
            for p in range(2):
                parts += [halo[0, p, w, :, cut], own_ref[p, w, :, cut], halo[1, p, w, :, cut]]
                parts += [blank[:, cut]]
            return jnp.concatenate(parts, axis=0)

        filter_window(bank_ref.shape[1], w, x, toep, index_ref, filt, power)
        white = whiten_window(w, band, mask_ref, filt, power)
        for p in range(2):
            out_ref[p, w] = white[p]
            mine[w, p] = white[p]
        for j in range(w // half, 2 * cols, 2):

            @pl.when(place != j)
            def _(j=j, w=w):
                beside_copy(place, j, w).start()

    for w in range(half):
        beside[place, w] = mine[core * half + w]

    count = line.count
    per = count // half

    def done_copy(k):
        return pltpu.make_async_remote_copy(
            src_ref=done.at[k],
            dst_ref=other.at[k],
            send_sem=done_sems.at[0, k],
            recv_sem=done_sems.at[1, k],
            device_id={"chan": partner},
            device_id_type=mesh_id,
        )

    @pl.loop(0, count + LAG * (rows - 1))
    def _(t):
        @pl.when(t < count)
        def _():
            w = t // per

            @pl.when(t % per == 0)
            def _():
                for j in range(2 * cols):

                    @pl.when(place != j)
                    def _(j=j):
                        beside_copy(j, j, w).wait_recv()

            r, p = (t % per) // 2, t % 2
            total = jnp.zeros((chans, bins), bf16)
            for j in range(2 * cols):
                total += beside[j, w, p] * (owner_ref[r] == base + j).astype(f32).astype(bf16)
            line.own[t] = total

        line.tick(t)
        k = t - LAG * (rows - 1)

        @pl.when(k >= 0)
        def _():
            total = line.result(k)
            done[k] = total
            done_copy(k).start()
            src_ref[(k % per) // 2, k % 2, core * half + k // per] = total

    @pl.loop(0, count)
    def _(k):
        done_copy(k).wait_recv()
        src_ref[(k % per) // 2, k % 2, (1 - core) * half + k // per] = other[k]

    for way in range(2):
        for w in range(wins):

            @pl.when(sends[way])
            def _(way=way, w=w):
                halo_copy(way, w).wait_send()

    for w in range(wins):
        for j in range(w // half, 2 * cols, 2):

            @pl.when(place != j)
            def _(j=j, w=w):
                beside_copy(place, j, w).wait_send()

    line.drain()

    @pl.loop(0, count)
    def _(k):
        done_copy(k).wait_send()


def front(grid, owner, own, bank, index, mask):
    _, wins, chans, bins = own.shape
    nbank = bank.shape[1]
    rounds = owner.shape[0]
    rows, cols = grid
    half = wins // 2
    count = rounds * half * 2
    vmem = pl.BlockSpec(memory_space=pltpu.VMEM)
    chunk = (chans, bins)
    chunks = pltpu.VMEM((count, *chunk), bf16)
    return pl.pallas_call(
        functools.partial(front_kernel, rows, cols),
        out_shape=[
            jax.ShapeDtypeStruct(own.shape, bf16),
            jax.ShapeDtypeStruct((rounds, *own.shape), bf16),
        ],
        in_specs=[pl.BlockSpec(memory_space=pltpu.SMEM)] + [vmem] * 4,
        out_specs=[vmem] * 2,
        scratch_shapes=[
            pltpu.VMEM((2, *own.shape), bf16),
            pltpu.VMEM((2, nbank * 2 * chans, 2 * LANES), bf16),
            pltpu.VMEM((bins, bins), bf16),
            pltpu.VMEM((2, wins * chans, bins), f32),
            pltpu.VMEM((2, wins * chans, bins), bf16),
            pltpu.VMEM((wins, 2, *chunk), bf16),
            pltpu.VMEM((2 * cols, half, 2, *chunk), bf16),
            [chunks] * 5,
            chunks,
            chunks,
            pltpu.SemaphoreType.DMA((2, 2, wins)),
            pltpu.SemaphoreType.DMA((2, 2 * cols, half)),
            pltpu.SemaphoreType.DMA((2, 2, count)),
            pltpu.SemaphoreType.DMA((2, count)),
        ],
        compiler_params=pltpu.CompilerParams(collective_id=0, has_side_effects=True),
        name="front",
    )(owner, own, bank, index, mask)


def tree_sum(terms):
    while len(terms) > 1:
        terms = [a + b for a, b in zip(terms[::2], terms[1::2])]
    return terms[0]


def cross_kernel(offset_ref, src_ref, loc_ref, out_ref, wide):
    _, wins, chans, bins = loc_ref.shape
    count = out_ref.shape[1]
    r, h = pl.program_id(0), pl.program_id(1)

    @pl.when(h == 0)
    def _():
        for p in range(2):
            for w in range(wins):
                wide[:, p * wins + w, :] = src_ref[0, p, w].astype(f32) * (1.0 / wins)

    for n in range(bins // LANES):
        cut = slice(n * LANES, (n + 1) * LANES)
        loc = [[loc_ref[p, w, :, cut] for w in range(wins)] for p in range(2)]

        def one(j, carry, cut=cut, loc=loc):
            at = offset_ref[r, h * count + j]
            src = [
                [
                    jnp.broadcast_to(
                        wide[at, p * wins + w : p * wins + w + 1, cut], (chans, LANES)
                    ).astype(bf16)
                    for w in range(wins)
                ]
                for p in range(2)
            ]
            real = tree_sum(
                [src[p][w] * loc[p][w] for w in range(wins) for p in range(2)]
            )
            plus = tree_sum([src[0][w] * loc[1][w] for w in range(wins)])
            minus = tree_sum([src[1][w] * loc[0][w] for w in range(wins)])
            out_ref[0, j, :, cut] = real
            out_ref[1, j, :, cut] = plus - minus
            return carry

        lax.fori_loop(0, count, one, 0, unroll=4)


def cross(offset, src, loc, blocks=2):
    rounds, _, wins, chans, bins = src.shape
    per = chans // blocks
    return pl.pallas_call(
        cross_kernel,
        out_shape=jax.ShapeDtypeStruct((2, rounds * chans, chans, bins), bf16),
        grid=(rounds, blocks),
        in_specs=[
            pl.BlockSpec(memory_space=pltpu.SMEM),
            pl.BlockSpec((1, 2, wins, chans, bins), lambda r, h: (r, 0, 0, 0, 0)),
            pl.BlockSpec((2, wins, chans, bins), lambda r, h: (0, 0, 0, 0)),
        ],
        out_specs=pl.BlockSpec((2, per, chans, bins), lambda r, h: (0, r * blocks + h, 0, 0)),
        scratch_shapes=[pltpu.VMEM((chans, 2 * wins, bins), f32)],
        name="cross",
    )(offset, src, loc)


def chip_grid(size):
    chips = size // 2
    cols = 1
    while cols * cols * 4 <= chips:
        cols *= 2
    return chips // cols, cols


def body(spectra, filter_bank, band_index, window_mask, owner_order, source_offset):
    grid = chip_grid(lax.axis_size("chan"))
    whitened, sources = front(
        grid, owner_order, spectra, filter_bank, band_index[None, :], window_mask
    )
    return cross(source_offset, sources, whitened)


def solution(mesh):
    in_specs = (
        P(None, "groups", "chan", None),
        P(),
        P(),
        P("groups", "chan"),
        P("groups"),
        P("groups", None),
    )
    out_specs = P(None, "groups", "chan", None)
    return jax.shard_map(body, mesh=mesh, in_specs=in_specs, out_specs=out_specs, check_vma=False)
```

```python
import functools

import jax
import jax.numpy as jnp
from jax import lax
from jax.experimental import pallas as pl
from jax.experimental.pallas import tpu as pltpu
from jax.sharding import PartitionSpec as P

SMOOTH = 17
water_level = 0.05
bf16 = jnp.bfloat16
f32 = jnp.float32
LANES = 128
LAG = 4


def split(x):
    hi = x.astype(bf16)
    return hi, (x - hi.astype(f32)).astype(bf16)


def build_toeplitz(bank_ref, toep):
    _, nbank, ntap = bank_ref.shape
    chans = toep.shape[1] // (2 * nbank)
    for b in range(nbank):
        parts = []
        for p in range(2):
            row = jnp.concatenate(
                [bank_ref[p, b : b + 1, :], jnp.zeros((1, LANES - ntap), f32)], axis=1
            )
            full = jnp.broadcast_to(row, (chans, LANES))
            parts.append(split(pltpu.roll(full, 0, 1, stride=1, stride_axis=0)))
        at = b * 2 * chans
        for part in range(2):
            real, imag = parts[0][part], parts[1][part]
            toep[part, at : at + chans, :LANES] = real
            toep[part, at : at + chans, LANES:] = -imag
            toep[part, at + chans : at + 2 * chans, :LANES] = imag
            toep[part, at + chans : at + 2 * chans, LANES:] = real


def build_window(band):
    bins = band.shape[0]
    rows = lax.broadcasted_iota(jnp.int32, (bins, bins), 0)
    cols = lax.broadcasted_iota(jnp.int32, (bins, bins), 1)
    band[...] = (jnp.abs(rows - cols) <= SMOOTH // 2).astype(f32).astype(bf16)


def filter_window(nbank, w, x, toep, index_ref, filt, power):
    bins = filt.shape[2]
    chans = toep.shape[1] // (2 * nbank)
    tile = 256
    rows = slice(w * chans, (w + 1) * chans)
    for n in range(bins // tile):
        cut = slice(n * tile, (n + 1) * tile)
        here = x(cut)
        res = jnp.dot(toep[0], here, preferred_element_type=f32)
        res += jnp.dot(toep[1], here, preferred_element_type=f32)
        index = index_ref[:, cut]
        acc = res[: 2 * chans]
        for b in range(1, nbank):
            acc = jnp.where(index == b, res[2 * chans * b : 2 * chans * (b + 1)], acc)
        real, imag = acc[:chans], acc[chans:]
        filt[0, rows, cut] = real
        filt[1, rows, cut] = imag
        hi, lo = split(real * real + imag * imag)
        power[0, rows, cut] = hi
        power[1, rows, cut] = lo


def whiten_window(w, band, mask_ref, filt, power):
    chans = mask_ref.shape[1]
    rows = slice(w * chans, (w + 1) * chans)
    smooth = jnp.dot(power[0, rows], band[...], preferred_element_type=f32)
    smooth += jnp.dot(power[1, rows], band[...], preferred_element_type=f32)
    scale = lax.rsqrt(smooth * (1.0 / SMOOTH) + water_level)
    eye = lax.broadcasted_iota(jnp.int32, (chans, chans), 0) == lax.broadcasted_iota(
        jnp.int32, (chans, chans), 1
    )
    row = jnp.broadcast_to(mask_ref[w : w + 1, :].astype(f32), (chans, chans))
    valid = jnp.sum(jnp.where(eye, row, 0.0), axis=1, keepdims=True)
    scale = scale * valid
    return [(filt[p, rows] * scale).astype(bf16) for p in range(2)]


class Line:
    def __init__(self, pos, length, device_of, lag, refs):
        self.pos, self.length, self.device_of, self.lag = pos, length, device_of, lag
        self.own, self.out_r, self.out_l, self.in_r, self.in_l, self.sems = refs
        self.count = self.own.shape[0]

    def clear(self):
        @pl.when(self.pos == 0)
        def _():
            self.in_r[...] = jnp.zeros_like(self.in_r)

        @pl.when(self.pos == self.length - 1)
        def _():
            self.in_l[...] = jnp.zeros_like(self.in_l)

    def copy(self, way, k):
        out, into = (self.out_r, self.in_r) if way == 0 else (self.out_l, self.in_l)
        other = self.pos + 1 if way == 0 else self.pos - 1
        return pltpu.make_async_remote_copy(
            src_ref=out.at[k],
            dst_ref=into.at[k],
            send_sem=self.sems.at[way, 0, k],
            recv_sem=self.sems.at[way, 1, k],
            device_id={"chan": self.device_of(other)},
            device_id_type=pl.DeviceIdType.MESH,
        )

    def tick(self, t):
        for way in range(2):
            behind = self.pos if way == 0 else self.length - 1 - self.pos
            out, into = (self.out_r, self.in_r) if way == 0 else (self.out_l, self.in_l)
            k = t - self.lag * behind
            inside = jnp.logical_and(k >= 0, k < self.count)

            @pl.when(jnp.logical_and(inside, behind > 0))
            def _(way=way, k=k):
                self.copy(way, k).wait_recv()

            @pl.when(jnp.logical_and(inside, behind < self.length - 1))
            def _(way=way, k=k, out=out, into=into):
                out[k] = self.own[k] + into[k]
                self.copy(way, k).start()

    def result(self, k):
        return self.own[k] + self.in_r[k] + self.in_l[k]

    def drain(self):
        for way in range(2):
            behind = self.pos if way == 0 else self.length - 1 - self.pos

            @pl.when(behind < self.length - 1)
            def _(way=way):
                @pl.loop(0, self.count)
                def _(k):
                    self.copy(way, k).wait_send()


def front_kernel(
    rows,
    cols,
    owner_ref,
    own_ref,
    bank_ref,
    index_ref,
    mask_ref,
    out_ref,
    src_ref,
    halo,
    toep,
    band,
    filt,
    power,
    mine,
    beside,
    row_buf,
    done,
    gathered,
    halo_sems,
    beside_sems,
    row_sems,
    gather_sems,
):
    wins, chans = mask_ref.shape
    bins = own_ref.shape[3]
    parts = 2 * cols
    subs, piece = beside.shape[1], beside.shape[2]
    me = lax.axis_index("chan")
    size = rows * cols * 2
    core = me % 2
    place = me % (2 * cols)
    base = me - place
    row = me // (2 * cols)
    partner = me + 1 - 2 * core
    mesh_id = pl.DeviceIdType.MESH

    barrier = pltpu.get_barrier_semaphore()
    partners = [
        (me > 0, me - 1),
        (me < size - 1, me + 1),
        (row > 0, me - 2 * cols),
        (row < rows - 1, me + 2 * cols),
    ] + [(place != j, base + j) for j in range(2 * cols)]
    expected = jnp.int32(0)
    for there, who in partners:
        expected += there.astype(jnp.int32)

        @pl.when(there)
        def _(who=who):
            pl.semaphore_signal(barrier, inc=1, device_id={"chan": who}, device_id_type=mesh_id)

    pl.semaphore_wait(barrier, expected)

    def halo_copy(way, w):
        return pltpu.make_async_remote_copy(
            src_ref=own_ref.at[:, w],
            dst_ref=halo.at[way, :, w],
            send_sem=halo_sems.at[way, 0, w],
            recv_sem=halo_sems.at[way, 1, w],
            device_id={"chan": me + 1 - 2 * way},
            device_id_type=mesh_id,
        )

    order = list(range(wins))
    sends = (me < size - 1, me > 0)
    for w in order:
        for way in range(2):

            @pl.when(sends[way])
            def _(way=way, w=w):
                halo_copy(way, w).start()

    for way in range(2):

        @pl.when(jnp.logical_not(sends[1 - way]))
        def _(way=way):
            halo[way] = jnp.zeros_like(halo[way])

    line = Line(row, rows, lambda i: i * 2 * cols + place, LAG, (*row_buf, row_sems))
    line.clear()
    build_toeplitz(bank_ref, toep)
    build_window(band)

    def beside_copy(sender, j):
        return pltpu.make_async_remote_copy(
            src_ref=mine.at[pl.ds(j * subs, subs)],
            dst_ref=beside.at[sender],
            send_sem=beside_sems.at[0, j],
            recv_sem=beside_sems.at[1, sender],
            device_id={"chan": base + j},
            device_id_type=mesh_id,
        )

    blank = jnp.zeros((LANES - 3 * chans, bins), bf16)
    for w in order:
        for way in range(2):

            @pl.when(sends[1 - way])
            def _(way=way, w=w):
                halo_copy(way, w).wait_recv()

        def x(cut, w=w):
            stack = []
            for p in range(2):
                stack += [halo[0, p, w, :, cut], own_ref[p, w, :, cut], halo[1, p, w, :, cut]]
                stack += [blank[:, cut]]
            return jnp.concatenate(stack, axis=0)

        filter_window(bank_ref.shape[1], w, x, toep, index_ref, filt, power)
        white = whiten_window(w, band, mask_ref, filt, power)
        for p in range(2):
            out_ref[p, w] = white[p]
            for i in range(chans // piece):
                mine[(w * 2 + p) * (chans // piece) + i] = white[p][i * piece : (i + 1) * piece]
        for j in range(w * parts // wins, (w + 1) * parts // wins):

            @pl.when(place != j)
            def _(j=j):
                beside_copy(place, j).start()

    beside[place] = mine[pl.ds(place * subs, subs)]
    for j in range(parts):

        @pl.when(place != j)
        def _(j=j):
            beside_copy(j, j).wait_recv()

    count = line.count

    @pl.loop(0, count)
    def _(k):
        total = jnp.zeros((piece, bins), bf16)
        for j in range(parts):
            total += beside[j, k % subs] * (owner_ref[k // subs] == base + j).astype(f32).astype(bf16)
        line.own[k] = total

    def give(src, origin, k, sem, who):
        return pltpu.make_async_remote_copy(
            src_ref=src,
            dst_ref=gathered.at[origin, k],
            send_sem=gather_sems.at[sem, k],
            recv_sem=gather_sems.at[2 * parts + origin, k],
            device_id={"chan": who},
            device_id_type=mesh_id,
        )

    def put(j, k, value):
        src_ref[k // subs, j * subs + k % subs] = value

    alike = [jnp.logical_and(place != j, core == j % 2) for j in range(parts)]
    last = LAG * (rows - 1)

    @pl.loop(0, count + last + LAG)
    def _(t):
        line.tick(t)
        k = t - last

        @pl.when(jnp.logical_and(k >= 0, k < count))
        def _():
            total = line.result(k)
            done[k] = total
            for j in range(parts):

                @pl.when(alike[j])
                def _(j=j):
                    give(done.at[k], place, k, j, base + j).start()

            give(done.at[k], place, k, parts + place, partner).start()
            put(place, k, total)

        q = t - last - LAG

        @pl.when(q >= 0)
        def _():
            for j in range(parts):

                @pl.when(alike[j])
                def _(j=j):
                    give(done.at[q], j, q, j, partner).wait_recv()
                    give(gathered.at[j, q], j, q, parts + j, partner).start()
                    put(j, q, gathered[j, q])

    @pl.loop(0, count)
    def _(k):
        for j in range(parts):

            @pl.when(core != j % 2)
            def _(j=j):
                give(done.at[k], j, k, j, partner).wait_recv()
                put(j, k, gathered[j, k])

    for way in range(2):
        for w in range(wins):

            @pl.when(sends[way])
            def _(way=way, w=w):
                halo_copy(way, w).wait_send()

    for j in range(parts):

        @pl.when(place != j)
        def _(j=j):
            beside_copy(place, j).wait_send()

    line.drain()

    @pl.loop(0, count)
    def _(k):
        give(done.at[k], place, k, parts + place, partner).wait_send()
        for j in range(parts):

            @pl.when(alike[j])
            def _(j=j):
                give(done.at[k], place, k, j, partner).wait_send()
                give(gathered.at[j, k], j, k, parts + j, partner).wait_send()


def front(grid, owner, own, bank, index, mask):
    _, wins, chans, bins = own.shape
    nbank = bank.shape[1]
    rounds = owner.shape[0]
    rows, cols = grid
    parts = 2 * cols
    total = wins * 2 * chans
    piece = min(chans, total // parts)
    subs = total // parts // piece
    count = rounds * subs
    vmem = pl.BlockSpec(memory_space=pltpu.VMEM)
    chunk = (piece, bins)
    chunks = pltpu.VMEM((count, *chunk), bf16)
    return pl.pallas_call(
        functools.partial(front_kernel, rows, cols),
        out_shape=[
            jax.ShapeDtypeStruct(own.shape, bf16),
            jax.ShapeDtypeStruct((rounds, parts * subs, piece, bins), bf16),
        ],
        in_specs=[pl.BlockSpec(memory_space=pltpu.SMEM)] + [vmem] * 4,
        out_specs=[vmem] * 2,
        scratch_shapes=[
            pltpu.VMEM((2, *own.shape), bf16),
            pltpu.VMEM((2, nbank * 2 * chans, 2 * LANES), bf16),
            pltpu.VMEM((bins, bins), bf16),
            pltpu.VMEM((2, wins * chans, bins), f32),
            pltpu.VMEM((2, wins * chans, bins), bf16),
            pltpu.VMEM((parts * subs, *chunk), bf16),
            pltpu.VMEM((parts, subs, *chunk), bf16),
            [chunks] * 5,
            chunks,
            pltpu.VMEM((parts, count, *chunk), bf16),
            pltpu.SemaphoreType.DMA((2, 2, wins)),
            pltpu.SemaphoreType.DMA((2, parts)),
            pltpu.SemaphoreType.DMA((2, 2, count)),
            pltpu.SemaphoreType.DMA((3 * parts, count)),
        ],
        compiler_params=pltpu.CompilerParams(collective_id=0, has_side_effects=True),
        name="front",
    )(owner, own, bank, index, mask)


def tree_sum(terms):
    while len(terms) > 1:
        terms = [a + b for a, b in zip(terms[::2], terms[1::2])]
    return terms[0]


def cross_kernel(offset_ref, src_ref, loc_ref, out_ref, wide, held):
    _, wins, chans, bins = loc_ref.shape
    count = out_ref.shape[1]
    r, h = pl.program_id(0), pl.program_id(1)

    @pl.when(jnp.logical_and(r == 0, h == 0))
    def _():
        held[...] = loc_ref[...]

    @pl.when(h == 0)
    def _():
        for p in range(2):
            for w in range(wins):
                wide[:, p * wins + w, :] = src_ref[0, w, p].astype(f32) * (1.0 / wins)

    for n in range(bins // LANES):
        cut = slice(n * LANES, (n + 1) * LANES)

        def one(j, carry, cut=cut):
            loc = [[held[p, w, :, cut] for w in range(wins)] for p in range(2)]
            at = offset_ref[r, h * count + j]
            src = [
                [
                    jnp.broadcast_to(
                        wide[at, p * wins + w : p * wins + w + 1, cut], (chans, LANES)
                    ).astype(bf16)
                    for w in range(wins)
                ]
                for p in range(2)
            ]
            real = tree_sum(
                [src[p][w] * loc[p][w] for w in range(wins) for p in range(2)]
            )
            plus = tree_sum([src[0][w] * loc[1][w] for w in range(wins)])
            minus = tree_sum([src[1][w] * loc[0][w] for w in range(wins)])
            out_ref[0, j, :, cut] = real
            out_ref[1, j, :, cut] = plus - minus
            return carry

        lax.fori_loop(0, count, one, 0, unroll=4)


def cross(offset, src, loc, blocks=2):
    rounds, wins, _, chans, bins = src.shape
    per = chans // blocks
    return pl.pallas_call(
        cross_kernel,
        out_shape=jax.ShapeDtypeStruct((2, rounds * chans, chans, bins), bf16),
        grid=(rounds, blocks),
        in_specs=[
            pl.BlockSpec(memory_space=pltpu.SMEM),
            pl.BlockSpec((1, wins, 2, chans, bins), lambda r, h: (r, 0, 0, 0, 0)),
            pl.BlockSpec((2, wins, chans, bins), lambda r, h: (0, 0, 0, 0)),
        ],
        out_specs=pl.BlockSpec((2, per, chans, bins), lambda r, h: (0, r * blocks + h, 0, 0)),
        scratch_shapes=[
            pltpu.VMEM((chans, 2 * wins, bins), f32),
            pltpu.VMEM((2, wins, chans, bins), bf16),
        ],
        name="cross",
    )(offset, src, loc)


def chip_grid(size):
    chips = size // 2
    cols = 1
    while cols * cols * 4 <= chips:
        cols *= 2
    return chips // cols, cols


def body(spectra, filter_bank, band_index, window_mask, owner_order, source_offset):
    grid = chip_grid(lax.axis_size("chan"))
    whitened, sources = front(
        grid, owner_order, spectra, filter_bank, band_index[None, :], window_mask
    )
    _, wins, chans, bins = spectra.shape
    sources = sources.reshape(sources.shape[0], wins, 2, chans, bins)
    return cross(source_offset, sources, whitened)


def solution(mesh):
    in_specs = (
        P(None, "groups", "chan", None),
        P(),
        P(),
        P("groups", "chan"),
        P("groups"),
        P("groups", None),
    )
    out_specs = P(None, "groups", "chan", None)
    return jax.shard_map(body, mesh=mesh, in_specs=in_specs, out_specs=out_specs, check_vma=False)
```

```python
import functools

import jax
import jax.numpy as jnp
from jax import lax
from jax.experimental import pallas as pl
from jax.experimental.pallas import tpu as pltpu
from jax.sharding import PartitionSpec as P

SMOOTH = 17
water_level = 0.05
bf16 = jnp.bfloat16
f32 = jnp.float32
LANES = 128
LAG = 4


def split(x):
    hi = x.astype(bf16)
    return hi, (x - hi.astype(f32)).astype(bf16)


def build_toeplitz(bank_ref, toep):
    _, nbank, ntap = bank_ref.shape
    chans = toep.shape[1] // (2 * nbank)
    for b in range(nbank):
        parts = []
        for p in range(2):
            row = jnp.concatenate(
                [bank_ref[p, b : b + 1, :], jnp.zeros((1, LANES - ntap), f32)], axis=1
            )
            full = jnp.broadcast_to(row, (chans, LANES))
            parts.append(split(pltpu.roll(full, 0, 1, stride=1, stride_axis=0)))
        at = b * 2 * chans
        for part in range(2):
            real, imag = parts[0][part], parts[1][part]
            toep[part, at : at + chans, :LANES] = real
            toep[part, at : at + chans, LANES:] = -imag
            toep[part, at + chans : at + 2 * chans, :LANES] = imag
            toep[part, at + chans : at + 2 * chans, LANES:] = real


def build_window(band):
    bins = band.shape[0]
    rows = lax.broadcasted_iota(jnp.int32, (bins, bins), 0)
    cols = lax.broadcasted_iota(jnp.int32, (bins, bins), 1)
    band[...] = (jnp.abs(rows - cols) <= SMOOTH // 2).astype(f32).astype(bf16)


def filter_window(nbank, w, x, toep, index_ref, filt, power):
    bins = filt.shape[2]
    chans = toep.shape[1] // (2 * nbank)
    tile = 256
    rows = slice(w * chans, (w + 1) * chans)
    for n in range(bins // tile):
        cut = slice(n * tile, (n + 1) * tile)
        here = x(cut)
        res = jnp.dot(toep[0], here, preferred_element_type=f32)
        res += jnp.dot(toep[1], here, preferred_element_type=f32)
        index = index_ref[:, cut]
        acc = res[: 2 * chans]
        for b in range(1, nbank):
            acc = jnp.where(index == b, res[2 * chans * b : 2 * chans * (b + 1)], acc)
        real, imag = acc[:chans], acc[chans:]
        filt[0, rows, cut] = real
        filt[1, rows, cut] = imag
        hi, lo = split(real * real + imag * imag)
        power[0, rows, cut] = hi
        power[1, rows, cut] = lo


def whiten_window(w, band, mask_ref, filt, power):
    chans = mask_ref.shape[1]
    rows = slice(w * chans, (w + 1) * chans)
    smooth = jnp.dot(power[0, rows], band[...], preferred_element_type=f32)
    smooth += jnp.dot(power[1, rows], band[...], preferred_element_type=f32)
    scale = lax.rsqrt(smooth * (1.0 / SMOOTH) + water_level)
    eye = lax.broadcasted_iota(jnp.int32, (chans, chans), 0) == lax.broadcasted_iota(
        jnp.int32, (chans, chans), 1
    )
    row = jnp.broadcast_to(mask_ref[w : w + 1, :].astype(f32), (chans, chans))
    valid = jnp.sum(jnp.where(eye, row, 0.0), axis=1, keepdims=True)
    scale = scale * valid
    return [(filt[p, rows] * scale).astype(bf16) for p in range(2)]


class Line:
    def __init__(self, pos, length, device_of, lag, refs):
        self.pos, self.length, self.device_of, self.lag = pos, length, device_of, lag
        self.own, self.out_r, self.out_l, self.in_r, self.in_l, self.sems = refs
        self.count = self.own.shape[0]

    def clear(self):
        @pl.when(self.pos == 0)
        def _():
            self.in_r[...] = jnp.zeros_like(self.in_r)

        @pl.when(self.pos == self.length - 1)
        def _():
            self.in_l[...] = jnp.zeros_like(self.in_l)

    def copy(self, way, k):
        out, into = (self.out_r, self.in_r) if way == 0 else (self.out_l, self.in_l)
        other = self.pos + 1 if way == 0 else self.pos - 1
        return pltpu.make_async_remote_copy(
            src_ref=out.at[k],
            dst_ref=into.at[k],
            send_sem=self.sems.at[way, 0, k],
            recv_sem=self.sems.at[way, 1, k],
            device_id={"chan": self.device_of(other)},
            device_id_type=pl.DeviceIdType.MESH,
        )

    def tick(self, t):
        for way in range(2):
            behind = self.pos if way == 0 else self.length - 1 - self.pos
            out, into = (self.out_r, self.in_r) if way == 0 else (self.out_l, self.in_l)
            k = t - self.lag * behind
            inside = jnp.logical_and(k >= 0, k < self.count)

            @pl.when(jnp.logical_and(inside, behind > 0))
            def _(way=way, k=k):
                self.copy(way, k).wait_recv()

            @pl.when(jnp.logical_and(inside, behind < self.length - 1))
            def _(way=way, k=k, out=out, into=into):
                out[k] = self.own[k] + into[k]
                self.copy(way, k).start()

    def result(self, k):
        return self.own[k] + self.in_r[k] + self.in_l[k]

    def drain(self):
        for way in range(2):
            behind = self.pos if way == 0 else self.length - 1 - self.pos

            @pl.when(behind < self.length - 1)
            def _(way=way):
                @pl.loop(0, self.count)
                def _(k):
                    self.copy(way, k).wait_send()


def front_kernel(
    rows,
    cols,
    owner_ref,
    own_ref,
    bank_ref,
    index_ref,
    mask_ref,
    out_ref,
    src_ref,
    halo,
    toep,
    band,
    filt,
    power,
    mine,
    beside,
    row_buf,
    done,
    gathered,
    halo_sems,
    beside_sems,
    row_sems,
    gather_sems,
):
    wins, chans = mask_ref.shape
    bins = own_ref.shape[3]
    parts = 2 * cols
    subs, piece = beside.shape[1], beside.shape[2]
    me = lax.axis_index("chan")
    size = rows * cols * 2
    core = me % 2
    place = me % (2 * cols)
    base = me - place
    row = me // (2 * cols)
    partner = me + 1 - 2 * core
    mesh_id = pl.DeviceIdType.MESH

    barrier = pltpu.get_barrier_semaphore()
    partners = [
        (me > 0, me - 1),
        (me < size - 1, me + 1),
        (row > 0, me - 2 * cols),
        (row < rows - 1, me + 2 * cols),
    ] + [(place != j, base + j) for j in range(2 * cols)]
    expected = jnp.int32(0)
    for there, who in partners:
        expected += there.astype(jnp.int32)

        @pl.when(there)
        def _(who=who):
            pl.semaphore_signal(barrier, inc=1, device_id={"chan": who}, device_id_type=mesh_id)

    pl.semaphore_wait(barrier, expected)

    def halo_copy(way, w):
        return pltpu.make_async_remote_copy(
            src_ref=own_ref.at[:, w],
            dst_ref=halo.at[way, :, w],
            send_sem=halo_sems.at[way, 0, w],
            recv_sem=halo_sems.at[way, 1, w],
            device_id={"chan": me + 1 - 2 * way},
            device_id_type=mesh_id,
        )

    order = list(range(wins))
    sends = (me < size - 1, me > 0)
    for w in order:
        for way in range(2):

            @pl.when(sends[way])
            def _(way=way, w=w):
                halo_copy(way, w).start()

    for way in range(2):

        @pl.when(jnp.logical_not(sends[1 - way]))
        def _(way=way):
            halo[way] = jnp.zeros_like(halo[way])

    line = Line(row, rows, lambda i: i * 2 * cols + place, LAG, (*row_buf, row_sems))
    line.clear()
    build_toeplitz(bank_ref, toep)
    build_window(band)

    def beside_copy(sender, j):
        return pltpu.make_async_remote_copy(
            src_ref=mine.at[pl.ds(j * subs, subs)],
            dst_ref=beside.at[sender],
            send_sem=beside_sems.at[0, j],
            recv_sem=beside_sems.at[1, sender],
            device_id={"chan": base + j},
            device_id_type=mesh_id,
        )

    blank = jnp.zeros((LANES - 3 * chans, bins), bf16)
    for w in order:
        for way in range(2):

            @pl.when(sends[1 - way])
            def _(way=way, w=w):
                halo_copy(way, w).wait_recv()

        def x(cut, w=w):
            stack = []
            for p in range(2):
                stack += [halo[0, p, w, :, cut], own_ref[p, w, :, cut], halo[1, p, w, :, cut]]
                stack += [blank[:, cut]]
            return jnp.concatenate(stack, axis=0)

        filter_window(bank_ref.shape[1], w, x, toep, index_ref, filt, power)
        white = whiten_window(w, band, mask_ref, filt, power)
        for p in range(2):
            out_ref[p, w] = white[p]
            for i in range(chans // piece):
                mine[(w * 2 + p) * (chans // piece) + i] = white[p][i * piece : (i + 1) * piece]
        for j in range(w * parts // wins, (w + 1) * parts // wins):

            @pl.when(place != j)
            def _(j=j):
                beside_copy(place, j).start()

    beside[place] = mine[pl.ds(place * subs, subs)]
    for j in range(parts):

        @pl.when(place != j)
        def _(j=j):
            beside_copy(j, j).wait_recv()

    count = line.count

    @pl.loop(0, count)
    def _(k):
        total = jnp.zeros((piece, bins), bf16)
        for j in range(parts):
            total += beside[j, k % subs] * (owner_ref[k // subs] == base + j).astype(f32).astype(bf16)
        line.own[k] = total

    def give(src, origin, k, sem, who):
        return pltpu.make_async_remote_copy(
            src_ref=src,
            dst_ref=gathered.at[origin, k],
            send_sem=gather_sems.at[sem, k],
            recv_sem=gather_sems.at[2 * parts + origin, k],
            device_id={"chan": who},
            device_id_type=mesh_id,
        )

    def put(j, k, value):
        src_ref[k // subs, j * subs + k % subs] = value

    alike = [jnp.logical_and(place != j, core == j % 2) for j in range(parts)]
    last = LAG * (rows - 1)

    @pl.loop(0, count + last + LAG)
    def _(t):
        line.tick(t)
        k = t - last

        @pl.when(jnp.logical_and(k >= 0, k < count))
        def _():
            total = line.result(k)
            done[k] = total
            for j in range(parts):

                @pl.when(alike[j])
                def _(j=j):
                    give(done.at[k], place, k, j, base + j).start()

            give(done.at[k], place, k, parts + place, partner).start()
            put(place, k, total)

        q = t - last - LAG

        @pl.when(q >= 0)
        def _():
            for j in range(parts):

                @pl.when(alike[j])
                def _(j=j):
                    give(done.at[q], j, q, j, partner).wait_recv()
                    give(gathered.at[j, q], j, q, parts + j, partner).start()
                    put(j, q, gathered[j, q])

    @pl.loop(0, count)
    def _(k):
        for j in range(parts):

            @pl.when(core != j % 2)
            def _(j=j):
                give(done.at[k], j, k, j, partner).wait_recv()
                put(j, k, gathered[j, k])

    for way in range(2):
        for w in range(wins):

            @pl.when(sends[way])
            def _(way=way, w=w):
                halo_copy(way, w).wait_send()

    for j in range(parts):

        @pl.when(place != j)
        def _(j=j):
            beside_copy(place, j).wait_send()

    line.drain()

    @pl.loop(0, count)
    def _(k):
        give(done.at[k], place, k, parts + place, partner).wait_send()
        for j in range(parts):

            @pl.when(alike[j])
            def _(j=j):
                give(done.at[k], place, k, j, partner).wait_send()
                give(gathered.at[j, k], j, k, parts + j, partner).wait_send()


def front(grid, owner, own, bank, index, mask):
    _, wins, chans, bins = own.shape
    nbank = bank.shape[1]
    rounds = owner.shape[0]
    rows, cols = grid
    parts = 2 * cols
    total = wins * 2 * chans
    piece = min(chans, total // parts)
    subs = total // parts // piece
    count = rounds * subs
    vmem = pl.BlockSpec(memory_space=pltpu.VMEM)
    chunk = (piece, bins)
    chunks = pltpu.VMEM((count, *chunk), bf16)
    return pl.pallas_call(
        functools.partial(front_kernel, rows, cols),
        out_shape=[
            jax.ShapeDtypeStruct(own.shape, bf16),
            jax.ShapeDtypeStruct((rounds, parts * subs, piece, bins), bf16),
        ],
        in_specs=[pl.BlockSpec(memory_space=pltpu.SMEM)] + [vmem] * 4,
        out_specs=[vmem] * 2,
        scratch_shapes=[
            pltpu.VMEM((2, *own.shape), bf16),
            pltpu.VMEM((2, nbank * 2 * chans, 2 * LANES), bf16),
            pltpu.VMEM((bins, bins), bf16),
            pltpu.VMEM((2, wins * chans, bins), f32),
            pltpu.VMEM((2, wins * chans, bins), bf16),
            pltpu.VMEM((parts * subs, *chunk), bf16),
            pltpu.VMEM((parts, subs, *chunk), bf16),
            [chunks] * 5,
            chunks,
            pltpu.VMEM((parts, count, *chunk), bf16),
            pltpu.SemaphoreType.DMA((2, 2, wins)),
            pltpu.SemaphoreType.DMA((2, parts)),
            pltpu.SemaphoreType.DMA((2, 2, count)),
            pltpu.SemaphoreType.DMA((3 * parts, count)),
        ],
        compiler_params=pltpu.CompilerParams(collective_id=0, has_side_effects=True),
        name="front",
    )(owner, own, bank, index, mask)


def tree_sum(terms):
    while len(terms) > 1:
        terms = [a + b for a, b in zip(terms[::2], terms[1::2])]
    return terms[0]


def cross_kernel(offset_ref, src_ref, loc_ref, out_ref, wide, held):
    _, wins, chans, bins = loc_ref.shape
    count = out_ref.shape[1]
    r, h = pl.program_id(0), pl.program_id(1)

    @pl.when(jnp.logical_and(r == 0, h == 0))
    def _():
        held[...] = loc_ref[...]

    @pl.when(h == 0)
    def _():
        for p in range(2):
            for w in range(wins):
                wide[:, p * wins + w, :] = src_ref[0, w, p].astype(f32) * (1.0 / wins)

    for n in range(bins // LANES):
        cut = slice(n * LANES, (n + 1) * LANES)

        def one(j, carry, cut=cut):
            loc = [[held[p, w, :, cut] for w in range(wins)] for p in range(2)]
            at = offset_ref[r, h * count + j]
            src = [
                [
                    jnp.broadcast_to(
                        wide[at, p * wins + w : p * wins + w + 1, cut], (chans, LANES)
                    ).astype(bf16)
                    for w in range(wins)
                ]
                for p in range(2)
            ]
            real = tree_sum(
                [src[p][w] * loc[p][w] for w in range(wins) for p in range(2)]
            )
            plus = tree_sum([src[0][w] * loc[1][w] for w in range(wins)])
            minus = tree_sum([src[1][w] * loc[0][w] for w in range(wins)])
            out_ref[0, j, :, cut] = real
            out_ref[1, j, :, cut] = plus - minus
            return carry

        lax.fori_loop(0, count, one, 0, unroll=4)


def cross(offset, src, loc, blocks=1):
    rounds, wins, _, chans, bins = src.shape
    per = chans // blocks
    return pl.pallas_call(
        cross_kernel,
        out_shape=jax.ShapeDtypeStruct((2, rounds * chans, chans, bins), bf16),
        grid=(rounds, blocks),
        in_specs=[
            pl.BlockSpec(memory_space=pltpu.SMEM),
            pl.BlockSpec((1, wins, 2, chans, bins), lambda r, h: (r, 0, 0, 0, 0)),
            pl.BlockSpec((2, wins, chans, bins), lambda r, h: (0, 0, 0, 0)),
        ],
        out_specs=pl.BlockSpec((2, per, chans, bins), lambda r, h: (0, r * blocks + h, 0, 0)),
        scratch_shapes=[
            pltpu.VMEM((chans, 2 * wins, bins), f32),
            pltpu.VMEM((2, wins, chans, bins), bf16),
        ],
        name="cross",
    )(offset, src, loc)


def chip_grid(size):
    chips = size // 2
    cols = 1
    while cols * cols * 4 <= chips:
        cols *= 2
    return chips // cols, cols


def body(spectra, filter_bank, band_index, window_mask, owner_order, source_offset):
    grid = chip_grid(lax.axis_size("chan"))
    whitened, sources = front(
        grid, owner_order, spectra, filter_bank, band_index[None, :], window_mask
    )
    _, wins, chans, bins = spectra.shape
    sources = sources.reshape(sources.shape[0], wins, 2, chans, bins)
    return cross(source_offset, sources, whitened)


def solution(mesh):
    in_specs = (
        P(None, "groups", "chan", None),
        P(),
        P(),
        P("groups", "chan"),
        P("groups"),
        P("groups", None),
    )
    out_specs = P(None, "groups", "chan", None)
    return jax.shard_map(body, mesh=mesh, in_specs=in_specs, out_specs=out_specs, check_vma=False)
```
